32 devices in a mesh: ka: 16 (over z, y, core), aux: 2 (over x).
Axes of the slice: x: 2, y: 2, z: 4, core: 2. Of those that a mesh axis runs over, the one named last changes fastest.
Arguments:
- coefficients: bfloat16 [16, 4096, 128], P('ka'), may hold values from -2.09375 to 2.09375
- triple: bfloat16 [64, 2, 64, 768], P('aux'), may hold values from -0.5 to 0.5
- neighbors: int32 [64, 2], P('aux'), may hold values from 0 to 63
- w_screened: bfloat16 [16, 768, 1536], P('ka', 'aux'), as said below
- partner: int32 [2, 16], replicated, may hold values from 0 to 15, each once within a row
- q_ids: int32 [2], replicated, may hold values from 0 to 15
Outputs:
- sigma: float32 [16, 64, 128], P('ka', 'aux')
The draws below stay inside these ranges and needn't reach their ends.
Inputs may be any that keep to these rules, and one draw needn't show every extreme that they name: Each stored w_screened is Hermitian: its real block is symmetric and its imaginary block antisymmetric.
All inputs are finite; a program needn't handle non-finite values.
Results may differ from the reference program's by a relative error of at most 0.0085.
Values may be sent and summed in bfloat16 or wider, within the bound.
A program may use at most 128 MiB of HBM per device.

```python
import math
import jax
import jax.numpy as jnp
from jax import lax

CELL_ATOMS = 64
ORBITALS_PER_ATOM = 64
AUX_ATOM = 12
SIGMA_BANDS = 64
OCCUPIED_BANDS = 16
NEIGH = 2
TRANSFERS = 2
ORB = 4096
NAUX = 768
NK = 16
QPTS = 16


def draw_w_screened(key, part):
    keys = jax.random.split(jax.random.fold_in(key, 31), QPTS)

    def single(subkey):
        first, second, third, fourth = jax.random.split(subkey, 4)
        sym_base = jax.random.normal(first, (NAUX, NAUX), jnp.float32)
        anti_base = jax.random.normal(second, (NAUX, NAUX), jnp.float32)
        magnitude = jax.random.uniform(third, (NAUX,), jnp.float32, 0.5, 1.5)
        signs = jnp.where(jax.random.bernoulli(fourth, 0.5, (NAUX,)), 1.0, -1.0)
        real_block = 0.6 * (sym_base + sym_base.T) / jnp.sqrt(2.0 * NAUX) + jnp.diag(magnitude * signs)
        imag_block = 0.6 * (anti_base - anti_base.T) / jnp.sqrt(2.0 * NAUX)
        return jnp.concatenate([real_block, imag_block], axis=1)
    return lax.map(single, keys).astype(jnp.bfloat16)


def with_ends(entries, rng, smallest, top_value):
    spot = [jax.random.randint(jax.random.fold_in(rng, axis), (), 0, length) for axis, length in enumerate(entries.shape)]
    longest = entries.shape.index(max(entries.shape))
    neighbour = spot[:longest] + [(spot[longest] + 1) % entries.shape[longest]] + spot[longest + 1:]
    return entries.at[tuple(spot)].set(smallest).at[tuple(neighbour)].set(top_value)


def levels(stream_key, extent, shards, smallest, largest):
    factor_of, own = 1.0, jax.random.fold_in(stream_key, 6)
    for axis_at, parts in shards:
        steps = jnp.exp(jax.random.uniform(jax.random.fold_in(own, axis_at), (parts,), jnp.float32, smallest / len(shards), largest / len(shards)))
        factor_of = factor_of * jnp.repeat(steps, extent[axis_at] // parts).reshape([-1 if axis == axis_at else 1 for axis in range(len(extent))])
    return factor_of


def bell_draw(stream_key, extent, deviation, most, pieces=(), kind=jnp.bfloat16):
    drawn = jax.random.normal(stream_key, extent, jnp.float32) * deviation
    if len(pieces) > 0:
        drawn = levels(stream_key, extent, pieces, -0.22, 0.18) * drawn
    return jnp.clip(drawn, min=-most, max=most).astype(kind)


def setup_inputs(seed: int = 0) -> dict:
    streams_of = jax.random.split(jax.random.key(seed), 7)
    coefficients = bell_draw(streams_of[0], (NK, ORB, 2 * SIGMA_BANDS), 0.35, 2.09375, ((0, 16),))
    triple = bell_draw(streams_of[1], (CELL_ATOMS, NEIGH, ORBITALS_PER_ATOM, AUX_ATOM * ORBITALS_PER_ATOM), (ORBITALS_PER_ATOM * NEIGH) ** -0.5, 0.5, ((0, 2),))
    neighbors = with_ends(jax.random.randint(streams_of[2], (CELL_ATOMS, NEIGH), 0, CELL_ATOMS), jax.random.fold_in(streams_of[2], 1), 0, CELL_ATOMS - 1).astype(jnp.int32)
    w_screened = draw_w_screened(jax.random.fold_in(streams_of[6], 71), 0)
    partner = jax.vmap(lambda own: jax.random.permutation(own, NK))(jax.random.split(streams_of[4], TRANSFERS)).reshape((TRANSFERS, NK)).astype(jnp.int32)
    q_ids = jax.random.randint(streams_of[5], (TRANSFERS,), 0, QPTS).astype(jnp.int32)
    return {"coefficients": coefficients, "triple": triple, "neighbors": neighbors, "w_screened": w_screened, "partner": partner, "q_ids": q_ids}


def reference(coefficients, triple, neighbors, w_screened, partner, q_ids):
    band_count = SIGMA_BANDS
    prefactor = -1.0 / math.sqrt(TRANSFERS * NAUX * OCCUPIED_BANDS)
    distant_coef_gathered = jnp.concatenate([coefficients[:, :, :OCCUPIED_BANDS], coefficients[:, :, SIGMA_BANDS:SIGMA_BANDS + OCCUPIED_BANDS]], axis=2)
    triple_wide = triple.astype(jnp.float32)

    def each_kpoint_values(kpoint_index):
        home_coefficients = coefficients[kpoint_index].reshape(CELL_ATOMS, ORBITALS_PER_ATOM, 2 * SIGMA_BANDS).astype(jnp.float32)
        blocks = jnp.zeros((2 * SIGMA_BANDS, 2 * SIGMA_BANDS), jnp.float32)
        for momentum_transfer in range(TRANSFERS):
            distant_coefficients = distant_coef_gathered[partner[momentum_transfer, kpoint_index]].reshape(CELL_ATOMS, ORBITALS_PER_ATOM, 2 * OCCUPIED_BANDS)
            neighbour_coef = jnp.take(distant_coefficients, neighbors, axis=0).astype(jnp.float32)
            pair_half = jnp.einsum('cjoy,cjox->cyx', neighbour_coef, triple_wide).astype(jnp.bfloat16)
            pair_half = pair_half.reshape(CELL_ATOMS, 2 * OCCUPIED_BANDS, AUX_ATOM, ORBITALS_PER_ATOM).astype(jnp.float32)
            combos = jnp.einsum('cix,cyai->cayx', home_coefficients, pair_half)
            real_part = combos[..., :OCCUPIED_BANDS, :band_count] + combos[..., OCCUPIED_BANDS:, band_count:]
            imag_part = combos[..., OCCUPIED_BANDS:, :band_count] - combos[..., :OCCUPIED_BANDS, band_count:]
            products = jnp.concatenate([real_part, imag_part], axis=-1).astype(jnp.bfloat16)
            products = products.reshape(NAUX, OCCUPIED_BANDS, 2 * SIGMA_BANDS)
            rotated = jnp.concatenate([-products[..., band_count:], products[..., :band_count]], axis=-1)
            stacked = jnp.concatenate([products, rotated], axis=0).reshape(2 * NAUX, OCCUPIED_BANDS * 2 * SIGMA_BANDS)
            weights = w_screened[q_ids[momentum_transfer]]
            screened = jnp.dot(weights, stacked, preferred_element_type=jnp.float32).astype(jnp.bfloat16)
            screened = screened.reshape(NAUX * OCCUPIED_BANDS, 2 * SIGMA_BANDS)
            left_side = products.reshape(NAUX * OCCUPIED_BANDS, 2 * SIGMA_BANDS)
            blocks = blocks + lax.dot_general(left_side, screened, (((0,), (0,)), ((), ())), preferred_element_type=jnp.float32)
        sigma_real = blocks[:band_count, :band_count] + blocks[band_count:, band_count:]
        sigma_imag = blocks[:band_count, band_count:] - blocks[band_count:, :band_count]
        return prefactor * jnp.concatenate([sigma_real, sigma_imag], axis=-1)
    return lax.map(each_kpoint_values, jnp.arange(NK, dtype=jnp.int32))
```

```python
import functools
import math

import jax
import jax.numpy as jnp
from jax import lax
from jax.experimental import pallas as pl
from jax.experimental.pallas import tpu as pltpu
from jax.sharding import PartitionSpec as P

AUX_ATOM = 12
OCC = 16
VMEM = pltpu.VMEM
SMEM = pltpu.SMEM


def bounce_kernel(n, transfers, partner_ref, src_ref, out_ref, spread, picked, s1, r1, s2, r2):
    me = lax.axis_index("ka")
    barrier = pltpu.get_barrier_semaphore()

    def greet(off, carry):
        dst = lax.rem(me + off, n)
        pl.semaphore_signal(
            barrier, inc=1, device_id={"ka": dst}, device_id_type=pl.DeviceIdType.MESH
        )
        return carry

    lax.fori_loop(1, n, greet, 0)
    pl.semaphore_wait(barrier, n - 1)

    def first(off):
        dst = lax.rem(me + off, n)
        return pltpu.make_async_remote_copy(
            src_ref=src_ref.at[dst],
            dst_ref=spread.at[me],
            send_sem=s1.at[off],
            recv_sem=r1.at[off],
            device_id={"ka": dst},
            device_id_type=pl.DeviceIdType.MESH,
        )

    def second(t, off):
        dst = lax.rem(me + off, n)
        return pltpu.make_async_remote_copy(
            src_ref=picked.at[t, dst],
            dst_ref=out_ref.at[t, me],
            send_sem=s2.at[t, off],
            recv_sem=r2.at[t, off],
            device_id={"ka": dst},
            device_id_type=pl.DeviceIdType.MESH,
        )

    def start_first(off, carry):
        first(off).start()
        return carry

    def wait_first(off, carry):
        first(off).wait()
        return carry

    lax.fori_loop(1, n, start_first, 0)
    spread[me] = src_ref[me]
    lax.fori_loop(1, n, wait_first, 0)
    for t in range(transfers):

        def pick(k, carry, t=t):
            picked[t, k] = spread[partner_ref[t, k]]
            return carry

        def start_second(off, carry, t=t):
            second(t, off).start()
            return carry

        lax.fori_loop(0, n, pick, 0)
        lax.fori_loop(1, n, start_second, 0)
        out_ref[t, me] = picked[t, me]
    for t in range(transfers):

        def wait_second(off, carry, t=t):
            second(t, off).wait()
            return carry

        lax.fori_loop(1, n, wait_second, 0)


def bounce(src, partner, transfers):
    n, rows, lanes = src.shape
    return pl.pallas_call(
        functools.partial(bounce_kernel, n, transfers),
        out_shape=jax.ShapeDtypeStruct((transfers, n, rows, lanes), src.dtype),
        in_specs=[pl.BlockSpec(memory_space=SMEM), pl.BlockSpec(memory_space=VMEM)],
        out_specs=pl.BlockSpec(memory_space=VMEM),
        scratch_shapes=[
            VMEM((n, rows, lanes), src.dtype),
            VMEM((transfers, n, rows, lanes), src.dtype),
            pltpu.SemaphoreType.DMA((n,)),
            pltpu.SemaphoreType.DMA((n,)),
            pltpu.SemaphoreType.DMA((transfers, n)),
            pltpu.SemaphoreType.DMA((transfers, n)),
        ],
        compiler_params=pltpu.CompilerParams(collective_id=0, has_side_effects=True),
        name="bounce",
    )(partner, src)


def far_kernel(coef_ref, out_ref):
    for p in range(out_ref.shape[0]):
        block = coef_ref[p * 128 : (p + 1) * 128, :].astype(jnp.float32).T
        half = block.shape[0] // 2
        out_ref[p, 0:OCC] = block[0:OCC].astype(jnp.bfloat16)
        out_ref[p, OCC : 2 * OCC] = block[half : half + OCC].astype(jnp.bfloat16)


def far_pairs(coef):
    orbitals, doubled = coef.shape
    per = 4
    return pl.pallas_call(
        far_kernel,
        grid=(orbitals // 128 // per,),
        out_shape=jax.ShapeDtypeStruct((orbitals // 128, 2 * OCC, 128), jnp.bfloat16),
        in_specs=[pl.BlockSpec((per * 128, doubled), lambda g: (g, 0))],
        out_specs=pl.BlockSpec((per, 2 * OCC, 128), lambda g: (g, 0, 0)),
        name="far_pairs",
    )(coef)


def pair_kernel(group, nb_ref, half_ref, far_ref, triple_ref, coef_ref, own_ref, part_ref, stage):
    step = pl.program_id(0)
    low = lax.broadcasted_iota(jnp.int32, (4 * OCC, 128), 1) < 64
    sign = jnp.where(lax.broadcasted_iota(jnp.int32, (64, 128), 1) < 64, 1.0, -1.0)
    zero = jnp.zeros((64, 128), jnp.bfloat16)
    for g in range(group):
        c = step * group + g
        n0 = nb_ref[c, 0]
        n1 = nb_ref[c, 1]
        x0 = far_ref[n0 % 2, n0 // 2]
        x1 = far_ref[1 - n1 % 2, n1 // 2]
        lhs = jnp.where(low, x0, x1)
        half = jnp.dot(lhs, triple_ref[g], preferred_element_type=jnp.float32)
        half = half.astype(jnp.bfloat16)
        top, bottom = half[: 2 * OCC], half[2 * OCC :]
        home = coef_ref[g].astype(jnp.float32)
        with_real = (home * sign).astype(jnp.bfloat16)
        with_imag = pltpu.roll(home, 64, 1).astype(jnp.bfloat16)
        rhs = jnp.concatenate(
            [
                jnp.concatenate([with_real, zero], axis=1),
                jnp.concatenate([zero, with_real], axis=1),
                jnp.concatenate([with_imag, zero], axis=1),
                jnp.concatenate([zero, with_imag], axis=1),
            ],
            axis=0,
        )
        rows = jnp.concatenate(
            [
                jnp.concatenate(
                    [top[:, s * 128 : (s + 1) * 128], bottom[:, s * 128 : (s + 1) * 128]], axis=1
                )
                for s in range(AUX_ATOM // 2)
            ],
            axis=0,
        )
        prod = jnp.dot(rows, rhs, preferred_element_type=jnp.float32)
        for s in range(AUX_ATOM // 2):
            for t in range(2):
                for b in range(2):
                    at = (g * AUX_ATOM + 2 * s + b) * OCC
                    r = s * 2 * OCC + t * OCC
                    stage[t, at : at + OCC, :] = prod[r : r + OCC, b * 128 : (b + 1) * 128]
    count = group * AUX_ATOM
    for t, out in enumerate((own_ref, part_ref)):
        for l in range(OCC):
            out[l] = stage[t, pl.ds(l, count, stride=OCC), :].astype(jnp.bfloat16)


def pair_products(far, triple, coef, neighbors, half):
    atoms = triple.shape[0]
    group = 4
    shape = jax.ShapeDtypeStruct((OCC, atoms * AUX_ATOM, 128), jnp.bfloat16)
    steps = atoms // group
    out_spec = pl.BlockSpec((OCC, group * AUX_ATOM, 128), lambda c, nb, h: (0, c, 0))
    return pl.pallas_call(
        functools.partial(pair_kernel, group),
        grid_spec=pltpu.PrefetchScalarGridSpec(
            num_scalar_prefetch=2,
            grid=(steps,),
            in_specs=[
                pl.BlockSpec(far.shape, lambda c, nb, h: (0, 0, 0, 0)),
                pl.BlockSpec((group,) + triple.shape[1:], lambda c, nb, h: (c, 0, 0)),
                pl.BlockSpec((group,) + coef.shape[1:], lambda c, nb, h: (h[0] * steps + c, 0, 0)),
            ],
            out_specs=[out_spec, out_spec],
            scratch_shapes=[VMEM((2, group * AUX_ATOM * OCC, 128), jnp.float32)],
        ),
        out_shape=[shape, shape],
        cost_estimate=pl.CostEstimate(
            flops=1_600_000_000, bytes_accessed=30_000_000, transcendentals=0
        ),
        name="pair_products",
    )(neighbors, half, far, triple, coef)


def screen_kernel(count, *refs):
    w_ref = refs[0]
    out_ref = refs[-1]
    rows = w_ref.shape[1] // 2

    @pl.when(pl.program_id(0) == 0)
    def _():
        out_ref[...] = jnp.zeros_like(out_ref)

    sign = jnp.where(lax.broadcasted_iota(jnp.int32, (rows, 128), 1) < 64, -1.0, 1.0)
    total = out_ref[...]
    for u in range(count):
        right, left = refs[1 + 2 * u], refs[2 + 2 * u]
        wide = jnp.concatenate([right[0], right[1]], axis=1)
        prod = jnp.dot(w_ref[u], wide, preferred_element_type=jnp.float32)
        for e in range(2):
            re = prod[:rows, e * 128 : (e + 1) * 128]
            im = prod[rows:, e * 128 : (e + 1) * 128]
            scr = (re + sign * pltpu.roll(im, 64, 1)).astype(jnp.bfloat16)
            total = total + lax.dot_general(
                left[e], scr, (((0,), (0,)), ((), ())), preferred_element_type=jnp.float32
            )
    out_ref[...] = total


def screen(weights, pairs, name):
    count = weights.shape[0]
    occ, rows, doubled = pairs[0][0].shape
    spec = pl.BlockSpec((2, rows, doubled), lambda s: (s, 0, 0))
    return pl.pallas_call(
        functools.partial(screen_kernel, count),
        grid=(occ // 2,),
        out_shape=jax.ShapeDtypeStruct((doubled, doubled), jnp.float32),
        in_specs=[pl.BlockSpec(weights.shape, lambda s: (0, 0, 0))] + [spec] * (2 * count),
        out_specs=pl.BlockSpec((doubled, doubled), lambda s: (0, 0)),
        cost_estimate=pl.CostEstimate(
            flops=count * 4_000_000_000, bytes_accessed=count * 10_000_000, transcendentals=0
        ),
        name=name,
    )(weights, *[x for pair in pairs for x in pair])


def swap(value, axis, mask):
    pairs = [(source, source ^ mask) for source in range(lax.axis_size(axis))]
    return lax.ppermute(value, axis, pairs)


def spread_root(value, axis):
    n = lax.axis_size(axis)
    me = lax.axis_index(axis)
    rows, cols = value.shape
    bits = [1 << b for b in range(n.bit_length() - 1)]
    for bit in bits:
        mine = (me // bit) % 2
        halves = value.reshape(2, value.shape[0] // 2, cols)
        kept = lax.dynamic_index_in_dim(halves, mine, 0, keepdims=False)
        sent = lax.dynamic_index_in_dim(halves, 1 - mine, 0, keepdims=False)
        value = kept + swap(sent, axis, bit)
    for bit in reversed(bits):
        mine = (me // bit) % 2
        other = swap(value, axis, bit)
        value = jnp.concatenate(
            [jnp.where(mine == 0, value, other), jnp.where(mine == 0, other, value)], axis=0
        )
    return value


def local(coefficients, triple, neighbors, w_screened, partner, q_ids):
    transfers = partner.shape[0]
    coef = coefficients[0]
    orbitals, doubled = coef.shape
    bands = doubled // 2
    atoms, neigh, per_atom, width = triple.shape
    aux_rows = atoms * AUX_ATOM
    naux = w_screened.shape[2] // 2
    n = lax.axis_size("ka")
    me = lax.axis_index("ka")
    half = lax.axis_index("aux")
    prefactor = -1.0 / math.sqrt(transfers * naux * OCC)

    order = jnp.stack([half, 1 - half])
    partner_here = jnp.take(partner, order, axis=0)
    q_here = jnp.take(q_ids, order, axis=0)

    weights = w_screened[0].reshape(aux_rows, 2, 2, aux_rows)
    own = lax.dynamic_index_in_dim(weights, half, 2, keepdims=False)
    other = lax.dynamic_index_in_dim(weights, 1 - half, 2, keepdims=False)
    own = jnp.moveaxis(own, 1, 0) * jnp.bfloat16(0.5)
    other = jnp.moveaxis(other, 1, 0)
    zero = jnp.zeros_like(own)
    first = me == q_here[0]
    second = me == q_here[1]
    payload = jnp.concatenate(
        [
            jnp.where(first, own, zero),
            jnp.where(second, own, zero),
            jnp.where(first, other, zero),
        ],
        axis=0,
    ).reshape(6 * aux_rows, aux_rows)
    payload = spread_root(payload, "ka").reshape(3, 2 * aux_rows, aux_rows)

    packed = far_pairs(coef)
    rows = packed.shape[0] * packed.shape[1]
    arrived = bounce(packed.reshape(n, rows // n, 128), partner_here, transfers)
    far = arrived.reshape(transfers, packed.shape[0], 2, OCC, 128)
    far = jnp.transpose(far, (1, 2, 0, 3, 4)).reshape(packed.shape[0], 2 * transfers * OCC, 128)
    far = jnp.stack([far, jnp.concatenate([far[..., 64:], far[..., :64]], axis=-1)])

    mine, part = pair_products(
        far,
        triple.reshape(atoms, neigh * per_atom, width),
        coef.reshape(orbitals // per_atom, per_atom, doubled),
        neighbors,
        half.astype(jnp.int32).reshape(1),
    )
    incoming = swap(part, "aux", 1)
    blocks = screen(payload[:2], [(mine, mine), (part, part)], "screen_own")
    blocks = blocks + screen(payload[2:], [(incoming, mine)], "screen_cross")
    real = blocks[:bands, :bands] + blocks[bands:, bands:]
    imag = blocks[:bands, bands:] - blocks[bands:, :bands]
    sigma = prefactor * jnp.concatenate([real + real.T, imag - imag.T], axis=-1)
    halves = sigma.reshape(2, bands // 2, doubled)
    sent = lax.dynamic_index_in_dim(halves, 1 - half, 0, keepdims=False)
    kept = lax.dynamic_index_in_dim(halves, half, 0, keepdims=False)
    return (kept + swap(sent, "aux", 1))[None]


def solution(mesh):
    in_specs = (
        P("ka", None, None),
        P("aux", None, None, None),
        P("aux", None),
        P("ka", "aux", None),
        P(),
        P(),
    )
    out_specs = P("ka", "aux", None)
    return jax.shard_map(local, mesh=mesh, in_specs=in_specs, out_specs=out_specs, check_vma=False)
```
